32 devices in a mesh: seq: 4 (over z), row: 2 (over core), col: 4 (over y, x).
Axes of the slice: x: 2, y: 2, z: 4, core: 2. Of those that a mesh axis runs over, the one named last changes fastest.
Arguments:
- query_input: bfloat16 [2048, 3072], P(('seq', 'row'), 'col'), may hold values from -6 to 6
- key_input: bfloat16 [2048, 3072], P(('seq', 'row'), 'col'), may hold values from -6 to 6
- value_input: bfloat16 [2048, 3072], P(('seq', 'row'), 'col'), may hold values from -6 to 6
- norm_gain: float32 [3072], P('col'), may hold values from 0.1 to 1.9
- out_weight: bfloat16 [3072, 6144], P(('seq', 'row'), 'col'), may hold values from -0.109375 to 0.109375
- out_grad: bfloat16 [2048, 6144], P(('seq', 'row'), 'col'), may hold values from -6 to 6
Outputs:
- projected: bfloat16 [2048, 6144], P(('seq', 'row'), 'col')
- query_grad: bfloat16 [2048, 3072], P(('seq', 'row'), 'col')
- key_grad: bfloat16 [2048, 3072], P(('seq', 'row'), 'col')
- value_grad: bfloat16 [2048, 3072], P(('seq', 'row'), 'col')
The draws below stay inside these ranges and needn't reach their ends.
All inputs are finite; a program needn't handle non-finite values.
Results may differ from the reference program's by a relative error of at most 0.0049.
Values may be sent and summed in bfloat16 or wider, within the bound.
No kernel may reach another device: no remote copies, remote signals or barrier semaphores. Data moves between devices by JAX's collectives and lax.ppermute only.
A program may use at most 128 MiB of HBM per device.

```python
import jax
import jax.numpy as jnp
from jax import lax

D = 6144
HEADS = 24
DH = 128
HG = 6
TOK_DEV = 256
HD = 3072
TOKENS = 2048


def block_levels(rng, dims, cuts, low, top_value):
    loudness, own = 1.0, jax.random.fold_in(rng, 6)
    for axis_at, parts in cuts:
        steps = jnp.exp(jax.random.uniform(jax.random.fold_in(own, axis_at), (parts,), jnp.float32, low / len(cuts), top_value / len(cuts)))
        loudness = loudness * jnp.repeat(steps, dims[axis_at] // parts).reshape([-1 if axis == axis_at else 1 for axis in range(len(dims))])
    return loudness


def gaussian(own_key, dims, deviation, bound, split=(), dtype=jnp.bfloat16):
    drawn = jax.random.normal(own_key, dims, jnp.float32) * deviation
    if len(split) > 0:
        drawn = block_levels(own_key, dims, split, -0.22, 0.18) * drawn
    return jnp.clip(drawn, min=-bound, max=bound).astype(dtype)


def setup_inputs(seed: int = 0) -> dict:
    key_of = jax.random.split(jax.random.key(seed), 7)
    query_input = gaussian(key_of[0], (TOKENS, HD), 1.0, 6.0, ((0, 8), (1, 4)))
    key_input = gaussian(key_of[1], (TOKENS, HD), 1.0, 6.0, ((0, 8), (1, 4)))
    value_input = gaussian(key_of[2], (TOKENS, HD), 1.0, 6.0, ((0, 8), (1, 4)))
    norm_gain = jnp.clip(1.0 + 0.18 * jax.random.normal(key_of[3], (HD,), jnp.float32), 0.1, 1.9)
    out_weight = gaussian(key_of[4], (HD, D), HD ** -0.5, 0.109375, ((0, 8), (1, 4)))
    out_grad = gaussian(key_of[5], (TOKENS, D), 1.0, 6.0, ((0, 8), (1, 4)))
    return {"query_input": query_input, "key_input": key_input, "value_input": value_input, "norm_gain": norm_gain, "out_weight": out_weight, "out_grad": out_grad}


norm_eps = 1e-05

def heads_view(matrix):
    return matrix.astype(jnp.float32).reshape(-1, TOK_DEV, HEADS, DH)

def reference(query_input, key_input, value_input, norm_gain, out_weight, out_grad):
    highest = lax.Precision.HIGHEST
    score_scale = DH ** (-0.5)
    queries = heads_view(query_input)
    key_vals = heads_view(key_input)
    value_vals = heads_view(value_input)
    positions = jnp.arange(TOK_DEV)
    causal = (positions[:, None] >= positions[None, :]).astype(jnp.float32)
    start_state = jnp.zeros((HEADS, DH, DH), jnp.float32)

    def forward_step(kv_state, block_in):
        query_blk, key_blk, value_blk = block_in
        scores = jnp.einsum('thd,shd->hts', query_blk, key_blk, precision=highest) * causal
        attend = jnp.einsum('hts,shd->thd', scores, value_blk, precision=highest)
        attend = attend + jnp.einsum('thd,hde->the', query_blk, kv_state, precision=highest)
        next_state = kv_state + jnp.einsum('tha,thb->hab', key_blk, value_blk, precision=highest)
        return (next_state, (attend * score_scale, kv_state))
    _, (attend, prefixes) = lax.scan(forward_step, start_state, (queries, key_vals, value_vals))
    attend = attend.reshape(TOKENS, HEADS // HG, HG * DH)
    inv_rms = lax.rsqrt(lax.optimization_barrier(jnp.mean(attend * attend, axis=-1, keepdims=True)) + norm_eps)
    normed = attend * inv_rms
    gain_groups = norm_gain.reshape(HEADS // HG, HG * DH)
    normalized = (normed * gain_groups).astype(jnp.bfloat16).reshape(TOKENS, HD)
    projected = jnp.dot(normalized, out_weight, preferred_element_type=jnp.float32).astype(jnp.bfloat16)
    grad_norm = lax.dot_general(out_grad, out_weight, (((1,), (1,)), ((), ())), preferred_element_type=jnp.float32)
    scaled = grad_norm.reshape(TOKENS, HEADS // HG, HG * DH) * gain_groups
    grad_attend = inv_rms * (scaled - normed * lax.optimization_barrier(jnp.mean(scaled * normed, axis=-1, keepdims=True)))
    grad_heads = grad_attend.reshape(-1, TOK_DEV, HEADS, DH)

    def backward_step(suffix, block_in):
        query_blk, key_blk, value_blk, grad_blk, prefix = block_in
        key_scores = jnp.einsum('thd,shd->hts', query_blk, key_blk, precision=highest) * causal
        value_scores = jnp.einsum('thd,shd->hts', grad_blk, value_blk, precision=highest) * causal
        query_part = jnp.einsum('hts,shd->thd', value_scores, key_blk, precision=highest)
        query_part = query_part + jnp.einsum('the,hde->thd', grad_blk, prefix, precision=highest)
        key_part = jnp.einsum('hts,thd->shd', value_scores, query_blk, precision=highest)
        key_part = key_part + jnp.einsum('shb,hab->sha', value_blk, suffix, precision=highest)
        value_part = jnp.einsum('hts,the->she', key_scores, grad_blk, precision=highest)
        value_part = value_part + jnp.einsum('sha,hab->shb', key_blk, suffix, precision=highest)
        next_state = suffix + jnp.einsum('tha,thb->hab', query_blk, grad_blk, precision=highest)
        return (next_state, (query_part * score_scale, key_part * score_scale, value_part * score_scale))
    _, grad_blocks = lax.scan(backward_step, start_state, (queries, key_vals, value_vals, grad_heads, prefixes), reverse=True)
    query_grad = grad_blocks[0].reshape(TOKENS, HD).astype(jnp.bfloat16)
    key_grad = grad_blocks[1].reshape(TOKENS, HD).astype(jnp.bfloat16)
    value_grad = grad_blocks[2].reshape(TOKENS, HD).astype(jnp.bfloat16)
    return (projected, query_grad, key_grad, value_grad)
```

```python
import jax
import jax.numpy as jnp
from jax import lax
from jax.sharding import PartitionSpec as P

DH = 128
HG = 6
CHUNK_HEADS = (1, 1, 1)

norm_eps = 1e-05
bf16 = jnp.bfloat16
f32 = jnp.float32


def carried_in(part, axis, reverse):
    count = lax.axis_size(axis)
    place = lax.axis_index(axis)
    gathered = lax.all_gather(part, axis)
    order = jnp.arange(count)
    keep = (order > place) if reverse else (order < place)
    return jnp.tensordot(keep.astype(f32), gathered, 1, precision=lax.Precision.HIGHEST)


def general(query_input, key_input, value_input, norm_gain, out_weight, out_grad):
    highest = lax.Precision.HIGHEST
    score_scale = DH ** (-0.5)
    tok_rows = query_input.shape[0]
    width_loc = query_input.shape[1]
    heads_loc = width_loc // DH
    groups_loc = heads_loc // HG
    query_heads = query_input.reshape(tok_rows, heads_loc, DH)
    key_heads = key_input.reshape(tok_rows, heads_loc, DH)
    value_heads = value_input.reshape(tok_rows, heads_loc, DH)
    query_float = query_heads.astype(f32)
    key_float = key_heads.astype(f32)
    value_float = value_heads.astype(f32)
    row_ids = lax.broadcasted_iota(jnp.int32, (tok_rows, tok_rows), 0)
    col_ids = lax.broadcasted_iota(jnp.int32, (tok_rows, tok_rows), 1)
    causal = (row_ids >= col_ids).astype(f32)
    own_kv = jnp.einsum("tha,thb->hab", key_heads, value_heads, preferred_element_type=f32)
    prefix = carried_in(own_kv, ("seq", "row"), False)
    key_scores = (
        jnp.einsum("thd,shd->hts", query_heads, key_heads, preferred_element_type=f32) * causal
    )
    attend = jnp.einsum("hts,shd->thd", key_scores, value_float, precision=highest)
    attend = attend + jnp.einsum("thd,hde->the", query_float, prefix, precision=highest)
    attend = (attend * score_scale).reshape(tok_rows, groups_loc, HG * DH)
    inv_rms = lax.rsqrt(jnp.mean(attend * attend, axis=-1, keepdims=True) + norm_eps)
    normed = attend * inv_rms
    gain_groups = norm_gain.reshape(groups_loc, HG * DH)
    normalized = (normed * gain_groups).astype(bf16).reshape(tok_rows, width_loc)
    weight_panel = lax.all_gather(out_weight, ("seq", "row"), axis=0, tiled=True)
    projected = jnp.dot(
        lax.all_gather(normalized, "col", axis=1, tiled=True),
        weight_panel,
        preferred_element_type=f32,
    )
    grad_parts = lax.dot_general(
        out_grad, weight_panel, (((1,), (1,)), ((), ())), preferred_element_type=f32
    )
    grad_norm = lax.psum_scatter(grad_parts, "col", scatter_dimension=1, tiled=True)
    scaled = grad_norm.reshape(tok_rows, groups_loc, HG * DH) * gain_groups
    grad_attend = inv_rms * (scaled - normed * jnp.mean(scaled * normed, axis=-1, keepdims=True))
    grad_heads = grad_attend.reshape(tok_rows, heads_loc, DH)
    own_qg = jnp.einsum("tha,thb->hab", query_float, grad_heads, precision=highest)
    suffix = carried_in(own_qg, ("seq", "row"), True)
    value_scores = jnp.einsum("thd,shd->hts", grad_heads, value_float, precision=highest) * causal
    query_part = jnp.einsum("hts,shd->thd", value_scores, key_float, precision=highest)
    query_part = query_part + jnp.einsum("the,hde->thd", grad_heads, prefix, precision=highest)
    key_part = jnp.einsum("hts,thd->shd", value_scores, query_float, precision=highest)
    key_part = key_part + jnp.einsum("shb,hab->sha", value_float, suffix, precision=highest)
    value_part = jnp.einsum("hts,the->she", key_scores, grad_heads, precision=highest)
    value_part = value_part + jnp.einsum("sha,hab->shb", key_float, suffix, precision=highest)
    query_grad = (query_part * score_scale).reshape(tok_rows, width_loc).astype(bf16)
    key_grad = (key_part * score_scale).reshape(tok_rows, width_loc).astype(bf16)
    value_grad = (value_part * score_scale).reshape(tok_rows, width_loc).astype(bf16)
    return (projected.astype(bf16), query_grad, key_grad, value_grad)


def row_swap(x):
    return lax.ppermute(x, "row", [(0, 1), (1, 0)])


def col_flip(x, bits):
    return lax.ppermute(x, "col", [(i, i ^ bits) for i in range(lax.axis_size("col"))])


def seq_shift(x, step):
    count = lax.axis_size("seq")
    return lax.ppermute(x, "seq", [(i, i + step) for i in range(count) if 0 <= i + step < count])


def seq_rotate(x):
    count = lax.axis_size("seq")
    return lax.ppermute(x, "seq", [(i, (i + 1) % count) for i in range(count)])


def sum_of_shifts(state, sign):
    sent = state.astype(bf16)
    total = jnp.zeros(state.shape, f32)
    for hop in range(1, lax.axis_size("seq")):
        total = total + seq_shift(sent, sign * hop).astype(f32)
    return total


def dot(spec, a, b):
    return jnp.einsum(spec, a.astype(bf16), b.astype(bf16), preferred_element_type=f32)


def head_split(query_input, key_input, value_input, norm_gain, out_weight, out_grad):
    score_scale = DH ** (-0.5)
    tok = query_input.shape[0]
    width = query_input.shape[1]
    half = width // 2
    heads = half // DH
    n_seq = lax.axis_size("seq")
    n_col = lax.axis_size("col")
    z = lax.axis_index("seq")
    r = lax.axis_index("row")
    c = lax.axis_index("col")

    held = []
    start = 0
    for count in CHUNK_HEADS:
        rows = count * DH
        blocks = [out_weight[start : start + rows]]
        for _ in range(n_seq - 1):
            blocks.append(seq_rotate(blocks[-1]))
        held.append(blocks)
        start += rows

    def halves_swapped(x):
        return jnp.concatenate([x[tok:], x[:tok]])

    def mine(x):
        return lax.dynamic_slice_in_dim(x, r * half, half, 1)

    def other(x):
        return lax.dynamic_slice_in_dim(x, (1 - r) * half, half, 1)

    qkv = (query_input, key_input, value_input)
    got = row_swap(jnp.stack([other(x) for x in qkv]))
    q, k, v = [
        jnp.concatenate([mine(x), got[i]], 0).reshape(2 * tok, heads, DH) for i, x in enumerate(qkv)
    ]
    grads = jnp.concatenate([out_grad, row_swap(out_grad)], 0)
    gain = lax.dynamic_slice_in_dim(norm_gain, r * half, half, 0)

    place = lax.broadcasted_iota(jnp.int32, (2 * tok, 1), 0)
    place = jnp.where(place < tok, place + r * tok, place - tok + (1 - r) * tok)
    causal = place >= place.reshape(1, 2 * tok)

    own_kv = dot("tha,thb->hab", k, v)
    prefix = sum_of_shifts(own_kv, 1)
    key_scores = jnp.where(causal, dot("thd,shd->hts", q, k), 0.0).astype(bf16)
    attend = dot("hts,shd->thd", key_scores, v) + dot("thd,hde->the", q, prefix)
    attend = attend.reshape(2 * tok, half) * score_scale
    squares = jnp.sum(attend * attend, axis=-1)
    squares = squares + halves_swapped(row_swap(squares))
    inv_rms = lax.rsqrt(squares * (1.0 / width) + norm_eps)[:, None]
    normed = attend * inv_rms
    normalized = (normed * gain).astype(bf16)

    pieces = []
    start = 0
    for count, blocks in zip(CHUNK_HEADS, held):
        parts = [
            lax.dot_general(grads, w, (((1,), (1,)), ((), ())), preferred_element_type=f32)
            for w in blocks
        ]

        def group(g):
            out = parts[0]
            for s in range(1, n_seq):
                out = jnp.where((z - g) % n_seq == s, parts[s], out)
            return out

        piece = group(c)
        for bits in range(1, n_col):
            piece = piece + col_flip(group(c ^ bits).astype(bf16), bits).astype(f32)
        pieces.append(piece)
        start += count
    grad_norm = jnp.concatenate(pieces, 1)

    feats = [normalized] + [col_flip(normalized, bits) for bits in range(1, n_col)]

    def features(g):
        out = feats[0]
        for bits in range(1, n_col):
            out = jnp.where(c ^ g == bits, feats[bits], out)
        return out

    partial = 0.0
    for s in range(n_seq):
        weight = jnp.concatenate([blocks[s] for blocks in held], 0)
        partial = partial + jnp.dot(
            features((z - s) % n_seq), weight, preferred_element_type=f32
        )
    projected = (partial[:tok] + row_swap(partial[tok:])).astype(bf16)

    scaled = grad_norm * gain
    inner = jnp.sum(scaled * normed, axis=-1)
    inner = (inner + halves_swapped(row_swap(inner)))[:, None] * (1.0 / width)
    grad_attend = inv_rms * (scaled - normed * inner)
    g = grad_attend.reshape(2 * tok, heads, DH).astype(bf16)

    suffix = sum_of_shifts(dot("tha,thb->hab", q, g), -1)
    value_scores = jnp.where(causal, dot("thd,shd->hts", g, v), 0.0).astype(bf16)
    query_part = dot("hts,shd->thd", value_scores, k) + dot("the,hde->thd", g, prefix)
    key_part = dot("hts,thd->shd", value_scores, q) + dot("shb,hab->sha", v, suffix)
    value_part = dot("hts,the->she", key_scores, g) + dot("sha,hab->shb", k, suffix)

    def settle(parts):
        whole = [(x * score_scale).reshape(2 * tok, half).astype(bf16) for x in parts]
        back = row_swap(jnp.stack([x[tok:] for x in whole]))
        return [
            jnp.where(
                r == 0,
                jnp.concatenate([x[:tok], y], 1),
                jnp.concatenate([y, x[:tok]], 1),
            )
            for x, y in zip(whole, back)
        ]

    (query_grad,) = settle([query_part])
    key_grad, value_grad = settle([key_part, value_part])
    return (projected, query_grad, key_grad, value_grad)


def solution(mesh):
    sizes = dict(mesh.shape)

    def per_device(query_input, key_input, value_input, norm_gain, out_weight, out_grad):
        width = query_input.shape[1]
        fits = (
            sizes["row"] == 2
            and sizes["seq"] == sizes["col"] == 4
            and width == HG * DH
            and 2 * out_weight.shape[0] == width
        )
        plan = head_split if fits else general
        return plan(query_input, key_input, value_input, norm_gain, out_weight, out_grad)

    in_specs = (
        P(("seq", "row"), "col"),
        P(("seq", "row"), "col"),
        P(("seq", "row"), "col"),
        P("col"),
        P(("seq", "row"), "col"),
        P(("seq", "row"), "col"),
    )
    out_specs = (
        P(("seq", "row"), "col"),
        P(("seq", "row"), "col"),
        P(("seq", "row"), "col"),
        P(("seq", "row"), "col"),
    )
    return jax.shard_map(
        per_device, mesh=mesh, in_specs=in_specs, out_specs=out_specs, check_vma=False
    )
```

```python
import jax
import jax.numpy as jnp
from jax import lax
from jax.experimental import pallas as pl
from jax.experimental.pallas import tpu as pltpu
from jax.sharding import PartitionSpec as P

DH = 128
HG = 6
CHUNK_HEADS = (1, 1, 1)

norm_eps = 1e-05
bf16 = jnp.bfloat16
f32 = jnp.float32


def carried_in(part, axis, reverse):
    count = lax.axis_size(axis)
    place = lax.axis_index(axis)
    gathered = lax.all_gather(part, axis)
    order = jnp.arange(count)
    keep = (order > place) if reverse else (order < place)
    return jnp.tensordot(keep.astype(f32), gathered, 1, precision=lax.Precision.HIGHEST)


def general(query_input, key_input, value_input, norm_gain, out_weight, out_grad):
    highest = lax.Precision.HIGHEST
    score_scale = DH ** (-0.5)
    tok_rows = query_input.shape[0]
    width_loc = query_input.shape[1]
    heads_loc = width_loc // DH
    groups_loc = heads_loc // HG
    query_heads = query_input.reshape(tok_rows, heads_loc, DH)
    key_heads = key_input.reshape(tok_rows, heads_loc, DH)
    value_heads = value_input.reshape(tok_rows, heads_loc, DH)
    query_float = query_heads.astype(f32)
    key_float = key_heads.astype(f32)
    value_float = value_heads.astype(f32)
    row_ids = lax.broadcasted_iota(jnp.int32, (tok_rows, tok_rows), 0)
    col_ids = lax.broadcasted_iota(jnp.int32, (tok_rows, tok_rows), 1)
    causal = (row_ids >= col_ids).astype(f32)
    own_kv = jnp.einsum("tha,thb->hab", key_heads, value_heads, preferred_element_type=f32)
    prefix = carried_in(own_kv, ("seq", "row"), False)
    key_scores = (
        jnp.einsum("thd,shd->hts", query_heads, key_heads, preferred_element_type=f32) * causal
    )
    attend = jnp.einsum("hts,shd->thd", key_scores, value_float, precision=highest)
    attend = attend + jnp.einsum("thd,hde->the", query_float, prefix, precision=highest)
    attend = (attend * score_scale).reshape(tok_rows, groups_loc, HG * DH)
    inv_rms = lax.rsqrt(jnp.mean(attend * attend, axis=-1, keepdims=True) + norm_eps)
    normed = attend * inv_rms
    gain_groups = norm_gain.reshape(groups_loc, HG * DH)
    normalized = (normed * gain_groups).astype(bf16).reshape(tok_rows, width_loc)
    weight_panel = lax.all_gather(out_weight, ("seq", "row"), axis=0, tiled=True)
    projected = jnp.dot(
        lax.all_gather(normalized, "col", axis=1, tiled=True),
        weight_panel,
        preferred_element_type=f32,
    )
    grad_parts = lax.dot_general(
        out_grad, weight_panel, (((1,), (1,)), ((), ())), preferred_element_type=f32
    )
    grad_norm = lax.psum_scatter(grad_parts, "col", scatter_dimension=1, tiled=True)
    scaled = grad_norm.reshape(tok_rows, groups_loc, HG * DH) * gain_groups
    grad_attend = inv_rms * (scaled - normed * jnp.mean(scaled * normed, axis=-1, keepdims=True))
    grad_heads = grad_attend.reshape(tok_rows, heads_loc, DH)
    own_qg = jnp.einsum("tha,thb->hab", query_float, grad_heads, precision=highest)
    suffix = carried_in(own_qg, ("seq", "row"), True)
    value_scores = jnp.einsum("thd,shd->hts", grad_heads, value_float, precision=highest) * causal
    query_part = jnp.einsum("hts,shd->thd", value_scores, key_float, precision=highest)
    query_part = query_part + jnp.einsum("the,hde->thd", grad_heads, prefix, precision=highest)
    key_part = jnp.einsum("hts,thd->shd", value_scores, query_float, precision=highest)
    key_part = key_part + jnp.einsum("shb,hab->sha", value_float, suffix, precision=highest)
    value_part = jnp.einsum("hts,the->she", key_scores, grad_heads, precision=highest)
    value_part = value_part + jnp.einsum("sha,hab->shb", key_float, suffix, precision=highest)
    query_grad = (query_part * score_scale).reshape(tok_rows, width_loc).astype(bf16)
    key_grad = (key_part * score_scale).reshape(tok_rows, width_loc).astype(bf16)
    value_grad = (value_part * score_scale).reshape(tok_rows, width_loc).astype(bf16)
    return (projected.astype(bf16), query_grad, key_grad, value_grad)


def row_swap(x):
    return lax.ppermute(x, "row", [(0, 1), (1, 0)])


def col_flip(x, bits):
    return lax.ppermute(x, "col", [(i, i ^ bits) for i in range(lax.axis_size("col"))])


def seq_shift(x, step):
    count = lax.axis_size("seq")
    return lax.ppermute(x, "seq", [(i, i + step) for i in range(count) if 0 <= i + step < count])


def seq_rotate(x):
    count = lax.axis_size("seq")
    return lax.ppermute(x, "seq", [(i, (i + 1) % count) for i in range(count)])


def shifts(state, sign):
    sent = state.astype(bf16)
    return [seq_shift(sent, sign * hop) for hop in range(1, lax.axis_size("seq"))]


def sum_of(parts):
    total = parts[0].astype(f32)
    for part in parts[1:]:
        total = total + part.astype(f32)
    return total


def dot(spec, a, b):
    return jnp.einsum(spec, a.astype(bf16), b.astype(bf16), preferred_element_type=f32)


class Fetch:
    def __init__(self, value):
        self.value = value


def block_of(shape):
    return pl.BlockSpec(tuple(shape), lambda: (0,) * len(shape))


def call(body, name, outs, place, ins, after=(), store=False):
    whole = pl.BlockSpec(memory_space=pltpu.VMEM)
    in_specs = [block_of(x.value.shape) if isinstance(x, Fetch) else whole for x in ins]
    ins = [x.value if isinstance(x, Fetch) else x for x in ins]
    anywhere = pl.BlockSpec(memory_space=pl.ANY)
    n_in, n_after = len(ins), len(after)

    def kernel(place_ref, *refs):
        body(place_ref, *refs[:n_in], *refs[n_in + n_after :])

    return pl.pallas_call(
        kernel,
        name=name,
        out_shape=[jax.ShapeDtypeStruct(shape, dtype) for shape, dtype in outs],
        in_specs=[pl.BlockSpec(memory_space=pltpu.SMEM)] + in_specs + [anywhere] * n_after,
        out_specs=[block_of(shape) if store else whole for shape, _ in outs],
        cost_estimate=pl.CostEstimate(flops=1, bytes_accessed=1, transcendentals=0),
        compiler_params=pltpu.CompilerParams(vmem_limit_bytes=40 * 2**20),
    )(place, *ins, *after)


def mm(a, b, ca, cb):
    return lax.dot_general(a, b, (((ca,), (cb,)), ((), ())), preferred_element_type=f32)


def half_of(ref, which, half):
    return ref[:, pl.ds(pl.multiple_of(which * half, DH), half)]


def head_of(ref, got, which, half, h):
    own = ref[:, pl.ds(pl.multiple_of(which * half + h * DH, DH), DH)]
    return jnp.concatenate([own, got[:, h * DH : (h + 1) * DH]], 0)


def swapped(x):
    tok = x.shape[0] // 2
    return jnp.concatenate([x[tok:], x[:tok]], 0)


def causal_mask(r, tok):
    def spot(axis):
        i = lax.broadcasted_iota(jnp.int32, (2 * tok, 2 * tok), axis)
        return jnp.where(i < tok, i + r * tok, i - r * tok)

    return spot(0) >= spot(1)


def total_of(parts, h):
    total = parts[0][h].astype(f32)
    for part in parts[1:]:
        total = total + part[h].astype(f32)
    return total.astype(bf16)


def head_split(query_input, key_input, value_input, norm_gain, out_weight, out_grad):
    score_scale = DH ** (-0.5)
    tok = query_input.shape[0]
    width = query_input.shape[1]
    half = width // 2
    heads = half // DH
    n_seq = lax.axis_size("seq")
    n_col = lax.axis_size("col")
    z = lax.axis_index("seq")
    r = lax.axis_index("row")
    c = lax.axis_index("col")

    held = []
    start = 0
    for count in CHUNK_HEADS:
        rows = count * DH
        blocks = [out_weight[start : start + rows]]
        for _ in range(n_seq - 1):
            blocks.append(seq_rotate(blocks[-1]))
        held.append(blocks)
        start += rows

    def halves_swapped(x):
        return jnp.concatenate([x[tok:], x[:tok]])

    def mine(x):
        return lax.dynamic_slice_in_dim(x, r * half, half, 1)

    def other(x):
        return lax.dynamic_slice_in_dim(x, (1 - r) * half, half, 1)

    qkv = (query_input, key_input, value_input)
    got = row_swap(jnp.stack([other(x) for x in qkv]))
    q, k, v = [
        jnp.concatenate([mine(x), got[i]], 0).reshape(2 * tok, heads, DH) for i, x in enumerate(qkv)
    ]
    grads = jnp.concatenate([out_grad, row_swap(out_grad)], 0)
    gain = lax.dynamic_slice_in_dim(norm_gain, r * half, half, 0)

    place = lax.broadcasted_iota(jnp.int32, (2 * tok, 1), 0)
    place = jnp.where(place < tok, place + r * tok, place - tok + (1 - r) * tok)
    causal = place >= place.reshape(1, 2 * tok)

    own_kv = dot("tha,thb->hab", k, v)
    prefix_parts = shifts(own_kv, 1)
    prefix = sum_of(prefix_parts)
    key_scores = jnp.where(causal, dot("thd,shd->hts", q, k), 0.0).astype(bf16)
    attend = dot("hts,shd->thd", key_scores, v) + dot("thd,hde->the", q, prefix)
    attend = attend.reshape(2 * tok, half) * score_scale
    squares = jnp.sum(attend * attend, axis=-1)
    squares = squares + halves_swapped(row_swap(squares))
    inv_rms = lax.rsqrt(squares * (1.0 / width) + norm_eps)[:, None]
    normed = attend * inv_rms
    normalized = (normed * gain).astype(bf16)

    pieces = []
    start = 0
    for count, blocks in zip(CHUNK_HEADS, held):
        parts = [
            lax.dot_general(grads, w, (((1,), (1,)), ((), ())), preferred_element_type=f32)
            for w in blocks
        ]

        def group(g):
            out = parts[0]
            for s in range(1, n_seq):
                out = jnp.where((z - g) % n_seq == s, parts[s], out)
            return out

        piece = group(c)
        for bits in range(1, n_col):
            piece = piece + col_flip(group(c ^ bits).astype(bf16), bits).astype(f32)
        pieces.append(piece)
        start += count

    feats = [normalized] + [col_flip(normalized, bits) for bits in range(1, n_col)]

    def features(g):
        out = feats[0]
        for bits in range(1, n_col):
            out = jnp.where(c ^ g == bits, feats[bits], out)
        return out

    partial = 0.0
    for s in range(n_seq):
        weight = jnp.concatenate([blocks[s] for blocks in held], 0)
        partial = partial + jnp.dot(
            features((z - s) % n_seq), weight, preferred_element_type=f32
        )
    scale = score_scale
    both = 2 * tok
    outs_loc = out_weight.shape[1]
    place = jnp.stack([z, r, c]).astype(jnp.int32)

    def scale_grad(s, *refs):
        grads, (gain, attend, inv_rms, scaled, inner) = refs[:heads], refs[heads:]
        total = 0.0
        for h in range(heads):
            cols = slice(h * DH, (h + 1) * DH)
            grad = grads[h][...] * gain[:, cols]
            scaled[:, cols] = grad
            normed = attend[:, cols] * inv_rms[...]
            total = total + jnp.sum(grad * normed, axis=1, keepdims=True)
        inner[...] = total

    scaled, inner = call(
        scale_grad,
        "scale_grad",
        [((both, half), f32), ((both, 1), f32)],
        place,
        [*pieces, gain.reshape(1, half), attend, inv_rms],
    )

    def back_state(s, scaled, inner, inner_got, attend, inv_rms, q, got, grad, state):
        mean = (inner[...] + swapped(inner_got[...])) * (1.0 / width)
        inv = inv_rms[...]
        value = (inv * (scaled[...] - attend[...] * inv * mean)).astype(bf16)
        grad[...] = value
        for h in range(heads):
            queries = head_of(q, got.at[0], s[1], half, h)
            state[h] = mm(queries, value[:, h * DH : (h + 1) * DH], 0, 0).astype(bf16)

    grad, state = call(
        back_state,
        "back_state",
        [((both, half), bf16), ((heads, DH, DH), bf16)],
        place,
        [scaled, inner, row_swap(inner), attend, inv_rms, query_input, got],
    )
    suffix = shifts(state, -1)

    def local_grads(s, q, k, v, got, grad, *refs):
        *prefix, dq_own, dq_other, own, other = refs
        mask = causal_mask(s[1], tok)
        for h in range(heads):
            cols = slice(h * DH, (h + 1) * DH)
            queries = head_of(q, got.at[0], s[1], half, h)
            keys = head_of(k, got.at[1], s[1], half, h)
            vals = head_of(v, got.at[2], s[1], half, h)
            grads = grad[:, cols]
            key_scores = jnp.where(mask, mm(queries, keys, 1, 1), 0.0).astype(bf16)
            value_scores = jnp.where(mask, mm(grads, vals, 1, 1), 0.0).astype(bf16)
            dq = mm(value_scores, keys, 1, 0) + mm(grads, total_of(prefix, h), 1, 1)
            dq = (dq * scale).astype(bf16)
            dq_own[:, cols] = dq[:tok]
            dq_other[:, cols] = dq[tok:]
            dk = mm(value_scores, queries, 0, 0)
            dv = mm(key_scores, grads, 0, 0)
            for i, x in enumerate((dk, dv)):
                own[i, :, cols] = x[:tok]
                other[i, :, cols] = x[tok:]

    dq_own, dq_other, kv_own, kv_other = call(
        local_grads,
        "local_grads",
        [((tok, half), bf16)] * 2 + [((2, tok, half), f32)] * 2,
        place,
        [query_input, key_input, value_input, got, grad, *prefix_parts],
    )
    kv_got = row_swap(kv_other)

    def finish_early(s, own, other, dq_own, dq_other, out, dq, token):
        token[...] = jnp.zeros_like(token)
        out[...] = (own[:tok] + other[...]).astype(bf16)
        dq[:, pl.ds(pl.multiple_of(s[1] * half, DH), half)] = dq_own[...]
        dq[:, pl.ds(pl.multiple_of((1 - s[1]) * half, DH), half)] = dq_other[...]

    projected, query_grad, token = call(
        finish_early,
        "finish_early",
        [((tok, outs_loc), bf16), ((tok, width), bf16), ((8, DH), f32)],
        place,
        [partial, row_swap(partial[tok:]), dq_own, row_swap(dq_other)],
        store=True,
    )

    def sum_later(s, *refs):
        *parts, _, total = refs
        for h in range(heads):
            total[h] = total_of(parts, h)

    (later,) = call(
        sum_later,
        "sum_later",
        [((heads, DH, DH), bf16)],
        place,
        [*suffix, token],
    )

    def far_grads(s, k, v, kv_own, kv_got, later, later_got, key_grad, value_grad):
        for local, state, which in ((kv_own, later, s[1]), (kv_got, later_got, 1 - s[1])):
            for h in range(heads):
                cols = slice(h * DH, (h + 1) * DH)
                place_cols = pl.ds(pl.multiple_of(which * half + h * DH, DH), DH)
                dk = local[0, :, cols] + mm(v[:, place_cols], state[h], 1, 1)
                dv = local[1, :, cols] + mm(k[:, place_cols], state[h], 1, 0)
                key_grad[:, place_cols] = (dk * scale).astype(bf16)
                value_grad[:, place_cols] = (dv * scale).astype(bf16)

    key_grad, value_grad = call(
        far_grads,
        "far_grads",
        [((tok, width), bf16)] * 2,
        place,
        [key_input, value_input, kv_own, kv_got, later, row_swap(later)],
        store=True,
    )
    return (projected, query_grad, key_grad, value_grad)


def solution(mesh):
    sizes = dict(mesh.shape)

    def per_device(query_input, key_input, value_input, norm_gain, out_weight, out_grad):
        width = query_input.shape[1]
        fits = (
            sizes["row"] == 2
            and sizes["seq"] == sizes["col"] == 4
            and width == HG * DH
            and 2 * out_weight.shape[0] == width
        )
        plan = head_split if fits else general
        return plan(query_input, key_input, value_input, norm_gain, out_weight, out_grad)

    in_specs = (
        P(("seq", "row"), "col"),
        P(("seq", "row"), "col"),
        P(("seq", "row"), "col"),
        P("col"),
        P(("seq", "row"), "col"),
        P(("seq", "row"), "col"),
    )
    out_specs = (
        P(("seq", "row"), "col"),
        P(("seq", "row"), "col"),
        P(("seq", "row"), "col"),
        P(("seq", "row"), "col"),
    )
    return jax.shard_map(
        per_device, mesh=mesh, in_specs=in_specs, out_specs=out_specs, check_vma=False
    )
```

```python
import jax
import jax.numpy as jnp
from jax import lax
from jax.experimental import pallas as pl
from jax.experimental.pallas import tpu as pltpu
from jax.sharding import PartitionSpec as P

DH = 128
HG = 6
CHUNK_HEADS = (1, 1, 1)

norm_eps = 1e-05
bf16 = jnp.bfloat16
f32 = jnp.float32


def carried_in(part, axis, reverse):
    count = lax.axis_size(axis)
    place = lax.axis_index(axis)
    gathered = lax.all_gather(part, axis)
    order = jnp.arange(count)
    keep = (order > place) if reverse else (order < place)
    return jnp.tensordot(keep.astype(f32), gathered, 1, precision=lax.Precision.HIGHEST)


def general(query_input, key_input, value_input, norm_gain, out_weight, out_grad):
    highest = lax.Precision.HIGHEST
    score_scale = DH ** (-0.5)
    tok_rows = query_input.shape[0]
    width_loc = query_input.shape[1]
    heads_loc = width_loc // DH
    groups_loc = heads_loc // HG
    query_heads = query_input.reshape(tok_rows, heads_loc, DH)
    key_heads = key_input.reshape(tok_rows, heads_loc, DH)
    value_heads = value_input.reshape(tok_rows, heads_loc, DH)
    query_float = query_heads.astype(f32)
    key_float = key_heads.astype(f32)
    value_float = value_heads.astype(f32)
    row_ids = lax.broadcasted_iota(jnp.int32, (tok_rows, tok_rows), 0)
    col_ids = lax.broadcasted_iota(jnp.int32, (tok_rows, tok_rows), 1)
    causal = (row_ids >= col_ids).astype(f32)
    own_kv = jnp.einsum("tha,thb->hab", key_heads, value_heads, preferred_element_type=f32)
    prefix = carried_in(own_kv, ("seq", "row"), False)
    key_scores = (
        jnp.einsum("thd,shd->hts", query_heads, key_heads, preferred_element_type=f32) * causal
    )
    attend = jnp.einsum("hts,shd->thd", key_scores, value_float, precision=highest)
    attend = attend + jnp.einsum("thd,hde->the", query_float, prefix, precision=highest)
    attend = (attend * score_scale).reshape(tok_rows, groups_loc, HG * DH)
    inv_rms = lax.rsqrt(jnp.mean(attend * attend, axis=-1, keepdims=True) + norm_eps)
    normed = attend * inv_rms
    gain_groups = norm_gain.reshape(groups_loc, HG * DH)
    normalized = (normed * gain_groups).astype(bf16).reshape(tok_rows, width_loc)
    weight_panel = lax.all_gather(out_weight, ("seq", "row"), axis=0, tiled=True)
    projected = jnp.dot(
        lax.all_gather(normalized, "col", axis=1, tiled=True),
        weight_panel,
        preferred_element_type=f32,
    )
    grad_parts = lax.dot_general(
        out_grad, weight_panel, (((1,), (1,)), ((), ())), preferred_element_type=f32
    )
    grad_norm = lax.psum_scatter(grad_parts, "col", scatter_dimension=1, tiled=True)
    scaled = grad_norm.reshape(tok_rows, groups_loc, HG * DH) * gain_groups
    grad_attend = inv_rms * (scaled - normed * jnp.mean(scaled * normed, axis=-1, keepdims=True))
    grad_heads = grad_attend.reshape(tok_rows, heads_loc, DH)
    own_qg = jnp.einsum("tha,thb->hab", query_float, grad_heads, precision=highest)
    suffix = carried_in(own_qg, ("seq", "row"), True)
    value_scores = jnp.einsum("thd,shd->hts", grad_heads, value_float, precision=highest) * causal
    query_part = jnp.einsum("hts,shd->thd", value_scores, key_float, precision=highest)
    query_part = query_part + jnp.einsum("the,hde->thd", grad_heads, prefix, precision=highest)
    key_part = jnp.einsum("hts,thd->shd", value_scores, query_float, precision=highest)
    key_part = key_part + jnp.einsum("shb,hab->sha", value_float, suffix, precision=highest)
    value_part = jnp.einsum("hts,the->she", key_scores, grad_heads, precision=highest)
    value_part = value_part + jnp.einsum("sha,hab->shb", key_float, suffix, precision=highest)
    query_grad = (query_part * score_scale).reshape(tok_rows, width_loc).astype(bf16)
    key_grad = (key_part * score_scale).reshape(tok_rows, width_loc).astype(bf16)
    value_grad = (value_part * score_scale).reshape(tok_rows, width_loc).astype(bf16)
    return (projected.astype(bf16), query_grad, key_grad, value_grad)


def row_swap(x):
    return lax.ppermute(x, "row", [(0, 1), (1, 0)])


def col_flip(x, bits):
    return lax.ppermute(x, "col", [(i, i ^ bits) for i in range(lax.axis_size("col"))])


def seq_shift(x, step):
    count = lax.axis_size("seq")
    return lax.ppermute(x, "seq", [(i, i + step) for i in range(count) if 0 <= i + step < count])


def seq_rotate(x):
    count = lax.axis_size("seq")
    return lax.ppermute(x, "seq", [(i, (i + 1) % count) for i in range(count)])


def shifts(state, sign):
    sent = state.astype(bf16)
    return [seq_shift(sent, sign * hop) for hop in range(1, lax.axis_size("seq"))]


def sum_of(parts):
    total = parts[0].astype(f32)
    for part in parts[1:]:
        total = total + part.astype(f32)
    return total


def dot(spec, a, b):
    return jnp.einsum(spec, a.astype(bf16), b.astype(bf16), preferred_element_type=f32)


class Fetch:
    def __init__(self, value):
        self.value = value


def block_of(shape):
    return pl.BlockSpec(tuple(shape), lambda: (0,) * len(shape))


def call(body, name, outs, place, ins, after=(), store=False):
    whole = pl.BlockSpec(memory_space=pltpu.VMEM)
    in_specs = [block_of(x.value.shape) if isinstance(x, Fetch) else whole for x in ins]
    ins = [x.value if isinstance(x, Fetch) else x for x in ins]
    anywhere = pl.BlockSpec(memory_space=pl.ANY)
    n_in, n_after = len(ins), len(after)

    def kernel(place_ref, *refs):
        body(place_ref, *refs[:n_in], *refs[n_in + n_after :])

    return pl.pallas_call(
        kernel,
        name=name,
        out_shape=[jax.ShapeDtypeStruct(shape, dtype) for shape, dtype in outs],
        in_specs=[pl.BlockSpec(memory_space=pltpu.SMEM)] + in_specs + [anywhere] * n_after,
        out_specs=[block_of(shape) if store else whole for shape, _ in outs],
        cost_estimate=pl.CostEstimate(flops=15 * 10**9 if name == "local_grads" else 1, bytes_accessed=1, transcendentals=0),
        compiler_params=pltpu.CompilerParams(vmem_limit_bytes=40 * 2**20),
    )(place, *ins, *after)


def mm(a, b, ca, cb):
    return lax.dot_general(a, b, (((ca,), (cb,)), ((), ())), preferred_element_type=f32)


def half_of(ref, which, half):
    return ref[:, pl.ds(pl.multiple_of(which * half, DH), half)]


def head_of(ref, got, which, half, h):
    own = ref[:, pl.ds(pl.multiple_of(which * half + h * DH, DH), DH)]
    return jnp.concatenate([own, got[:, h * DH : (h + 1) * DH]], 0)


def swapped(x):
    tok = x.shape[0] // 2
    return jnp.concatenate([x[tok:], x[:tok]], 0)


def causal_mask(r, tok):
    def spot(axis):
        i = lax.broadcasted_iota(jnp.int32, (2 * tok, 2 * tok), axis)
        return jnp.where(i < tok, i + r * tok, i - r * tok)

    return spot(0) >= spot(1)


def total_of(parts, h):
    total = parts[0][h].astype(f32)
    for part in parts[1:]:
        total = total + part[h].astype(f32)
    return total.astype(bf16)


def head_split(query_input, key_input, value_input, norm_gain, out_weight, out_grad):
    score_scale = DH ** (-0.5)
    tok = query_input.shape[0]
    width = query_input.shape[1]
    half = width // 2
    heads = half // DH
    n_seq = lax.axis_size("seq")
    n_col = lax.axis_size("col")
    z = lax.axis_index("seq")
    r = lax.axis_index("row")
    c = lax.axis_index("col")

    held = []
    start = 0
    for count in CHUNK_HEADS:
        rows = count * DH
        blocks = [out_weight[start : start + rows]]
        for _ in range(n_seq - 1):
            blocks.append(seq_rotate(blocks[-1]))
        held.append(blocks)
        start += rows

    def halves_swapped(x):
        return jnp.concatenate([x[tok:], x[:tok]])

    def mine(x):
        return lax.dynamic_slice_in_dim(x, r * half, half, 1)

    def other(x):
        return lax.dynamic_slice_in_dim(x, (1 - r) * half, half, 1)

    qkv = (query_input, key_input, value_input)
    got = row_swap(jnp.stack([other(x) for x in qkv]))
    q, k, v = [
        jnp.concatenate([mine(x), got[i]], 0).reshape(2 * tok, heads, DH) for i, x in enumerate(qkv)
    ]
    grads = jnp.concatenate([out_grad, row_swap(out_grad)], 0)
    gain = lax.dynamic_slice_in_dim(norm_gain, r * half, half, 0)

    place = lax.broadcasted_iota(jnp.int32, (2 * tok, 1), 0)
    place = jnp.where(place < tok, place + r * tok, place - tok + (1 - r) * tok)
    causal = place >= place.reshape(1, 2 * tok)

    own_kv = dot("tha,thb->hab", k, v)
    prefix_parts = shifts(own_kv, 1)
    prefix = sum_of(prefix_parts)
    key_scores = jnp.where(causal, dot("thd,shd->hts", q, k), 0.0).astype(bf16)
    attend = dot("hts,shd->thd", key_scores, v) + dot("thd,hde->the", q, prefix)
    attend = attend.reshape(2 * tok, half) * score_scale
    squares = jnp.sum(attend * attend, axis=-1)
    squares = squares + halves_swapped(row_swap(squares))
    inv_rms = lax.rsqrt(squares * (1.0 / width) + norm_eps)[:, None]
    normed = attend * inv_rms
    normalized = (normed * gain).astype(bf16)

    pieces = []
    start = 0
    for count, blocks in zip(CHUNK_HEADS, held):
        parts = [
            lax.dot_general(grads, w, (((1,), (1,)), ((), ())), preferred_element_type=f32)
            for w in blocks
        ]

        def group(g):
            out = parts[0]
            for s in range(1, n_seq):
                out = jnp.where((z - g) % n_seq == s, parts[s], out)
            return out

        piece = group(c)
        for bits in range(1, n_col):
            piece = piece + col_flip(group(c ^ bits).astype(bf16), bits).astype(f32)
        pieces.append(piece)
        start += count

    feats = [normalized] + [col_flip(normalized, bits) for bits in range(1, n_col)]

    def features(g):
        out = feats[0]
        for bits in range(1, n_col):
            out = jnp.where(c ^ g == bits, feats[bits], out)
        return out

    partial = 0.0
    for s in range(n_seq):
        weight = jnp.concatenate([blocks[s] for blocks in held], 0)
        partial = partial + jnp.dot(
            features((z - s) % n_seq), weight, preferred_element_type=f32
        )
    scale = score_scale
    both = 2 * tok
    outs_loc = out_weight.shape[1]
    place = jnp.stack([z, r, c]).astype(jnp.int32)

    def scale_grad(s, *refs):
        grads, (gain, attend, inv_rms, scaled, inner) = refs[:heads], refs[heads:]
        total = 0.0
        for h in range(heads):
            cols = slice(h * DH, (h + 1) * DH)
            grad = grads[h][...] * gain[:, cols]
            scaled[:, cols] = grad
            normed = attend[:, cols] * inv_rms[...]
            total = total + jnp.sum(grad * normed, axis=1, keepdims=True)
        inner[...] = total

    scaled, inner = call(
        scale_grad,
        "scale_grad",
        [((both, half), f32), ((both, 1), f32)],
        place,
        [*pieces, gain.reshape(1, half), attend, inv_rms],
    )

    def back_state(s, scaled, inner, inner_got, attend, inv_rms, q, got, grad, state):
        mean = (inner[...] + swapped(inner_got[...])) * (1.0 / width)
        inv = inv_rms[...]
        value = (inv * (scaled[...] - attend[...] * inv * mean)).astype(bf16)
        grad[...] = value
        for h in range(heads):
            queries = head_of(q, got.at[0], s[1], half, h)
            state[h] = mm(queries, value[:, h * DH : (h + 1) * DH], 0, 0).astype(bf16)

    grad, state = call(
        back_state,
        "back_state",
        [((both, half), bf16), ((heads, DH, DH), bf16)],
        place,
        [scaled, inner, row_swap(inner), attend, inv_rms, query_input, got],
    )
    suffix = shifts(state, -1)

    def local_grads(s, q, k, v, got, grad, *refs):
        *prefix, dq_own, dq_other, own, other = refs
        mask = causal_mask(s[1], tok)
        for h in range(heads):
            cols = slice(h * DH, (h + 1) * DH)
            queries = head_of(q, got.at[0], s[1], half, h)
            keys = head_of(k, got.at[1], s[1], half, h)
            vals = head_of(v, got.at[2], s[1], half, h)
            grads = grad[:, cols]
            key_scores = jnp.where(mask, mm(queries, keys, 1, 1), 0.0).astype(bf16)
            value_scores = jnp.where(mask, mm(grads, vals, 1, 1), 0.0).astype(bf16)
            dq = mm(value_scores, keys, 1, 0) + mm(grads, total_of(prefix, h), 1, 1)
            dq = (dq * scale).astype(bf16)
            dq_own[:, cols] = dq[:tok]
            dq_other[:, cols] = dq[tok:]
            dk = mm(value_scores, queries, 0, 0)
            dv = mm(key_scores, grads, 0, 0)
            for i, x in enumerate((dk, dv)):
                own[i, :, cols] = x[:tok]
                other[i, :, cols] = x[tok:]

    dq_own, dq_other, kv_own, kv_other = call(
        local_grads,
        "local_grads",
        [((tok, half), bf16)] * 2 + [((2, tok, half), f32)] * 2,
        place,
        [query_input, key_input, value_input, got, grad, *prefix_parts],
    )
    kv_got = row_swap(kv_other)

    def finish_early(s, own, other, dq_own, dq_other, out, dq, token):
        token[...] = jnp.zeros_like(token)
        out[...] = (own[:tok] + other[...]).astype(bf16)
        dq[:, pl.ds(pl.multiple_of(s[1] * half, DH), half)] = dq_own[...]
        dq[:, pl.ds(pl.multiple_of((1 - s[1]) * half, DH), half)] = dq_other[...]

    projected, query_grad, token = call(
        finish_early,
        "finish_early",
        [((tok, outs_loc), bf16), ((tok, width), bf16), ((8, DH), f32)],
        place,
        [partial, row_swap(partial[tok:]), dq_own, row_swap(dq_other)],
        store=True,
    )

    def sum_later(s, *refs):
        *parts, total = refs
        for h in range(heads):
            total[h] = total_of(parts, h)

    (later,) = call(
        sum_later,
        "sum_later",
        [((heads, DH, DH), bf16)],
        place,
        suffix,
    )

    def far_grads(s, k, v, kv_own, kv_got, later, later_got, token, key_grad, value_grad):
        for local, state, which in ((kv_own, later, s[1]), (kv_got, later_got, 1 - s[1])):
            for h in range(heads):
                cols = slice(h * DH, (h + 1) * DH)
                place_cols = pl.ds(pl.multiple_of(which * half + h * DH, DH), DH)
                dk = local[0, :, cols] + mm(v[:, place_cols], state[h], 1, 1)
                dv = local[1, :, cols] + mm(k[:, place_cols], state[h], 1, 0)
                key_grad[:, place_cols] = (dk * scale).astype(bf16)
                value_grad[:, place_cols] = (dv * scale).astype(bf16)

    key_grad, value_grad = call(
        far_grads,
        "far_grads",
        [((tok, width), bf16)] * 2,
        place,
        [key_input, value_input, kv_own, kv_got, later, row_swap(later), token],
        store=True,
    )
    return (projected, query_grad, key_grad, value_grad)


def solution(mesh):
    sizes = dict(mesh.shape)

    def per_device(query_input, key_input, value_input, norm_gain, out_weight, out_grad):
        width = query_input.shape[1]
        fits = (
            sizes["row"] == 2
            and sizes["seq"] == sizes["col"] == 4
            and width == HG * DH
            and 2 * out_weight.shape[0] == width
        )
        plan = head_split if fits else general
        return plan(query_input, key_input, value_input, norm_gain, out_weight, out_grad)

    in_specs = (
        P(("seq", "row"), "col"),
        P(("seq", "row"), "col"),
        P(("seq", "row"), "col"),
        P("col"),
        P(("seq", "row"), "col"),
        P(("seq", "row"), "col"),
    )
    out_specs = (
        P(("seq", "row"), "col"),
        P(("seq", "row"), "col"),
        P(("seq", "row"), "col"),
        P(("seq", "row"), "col"),
    )
    return jax.shard_map(
        per_device, mesh=mesh, in_specs=in_specs, out_specs=out_specs, check_vma=False
    )
```

```python
import jax
import jax.numpy as jnp
from jax import lax
from jax.experimental import pallas as pl
from jax.experimental.pallas import tpu as pltpu
from jax.sharding import PartitionSpec as P

DH = 128
HG = 6
CHUNK_HEADS = (1, 1, 1)

norm_eps = 1e-05
bf16 = jnp.bfloat16
f32 = jnp.float32


def carried_in(part, axis, reverse):
    count = lax.axis_size(axis)
    place = lax.axis_index(axis)
    gathered = lax.all_gather(part, axis)
    order = jnp.arange(count)
    keep = (order > place) if reverse else (order < place)
    return jnp.tensordot(keep.astype(f32), gathered, 1, precision=lax.Precision.HIGHEST)


def general(query_input, key_input, value_input, norm_gain, out_weight, out_grad):
    highest = lax.Precision.HIGHEST
    score_scale = DH ** (-0.5)
    tok_rows = query_input.shape[0]
    width_loc = query_input.shape[1]
    heads_loc = width_loc // DH
    groups_loc = heads_loc // HG
    query_heads = query_input.reshape(tok_rows, heads_loc, DH)
    key_heads = key_input.reshape(tok_rows, heads_loc, DH)
    value_heads = value_input.reshape(tok_rows, heads_loc, DH)
    query_float = query_heads.astype(f32)
    key_float = key_heads.astype(f32)
    value_float = value_heads.astype(f32)
    row_ids = lax.broadcasted_iota(jnp.int32, (tok_rows, tok_rows), 0)
    col_ids = lax.broadcasted_iota(jnp.int32, (tok_rows, tok_rows), 1)
    causal = (row_ids >= col_ids).astype(f32)
    own_kv = jnp.einsum("tha,thb->hab", key_heads, value_heads, preferred_element_type=f32)
    prefix = carried_in(own_kv, ("seq", "row"), False)
    key_scores = (
        jnp.einsum("thd,shd->hts", query_heads, key_heads, preferred_element_type=f32) * causal
    )
    attend = jnp.einsum("hts,shd->thd", key_scores, value_float, precision=highest)
    attend = attend + jnp.einsum("thd,hde->the", query_float, prefix, precision=highest)
    attend = (attend * score_scale).reshape(tok_rows, groups_loc, HG * DH)
    inv_rms = lax.rsqrt(jnp.mean(attend * attend, axis=-1, keepdims=True) + norm_eps)
    normed = attend * inv_rms
    gain_groups = norm_gain.reshape(groups_loc, HG * DH)
    normalized = (normed * gain_groups).astype(bf16).reshape(tok_rows, width_loc)
    weight_panel = lax.all_gather(out_weight, ("seq", "row"), axis=0, tiled=True)
    projected = jnp.dot(
        lax.all_gather(normalized, "col", axis=1, tiled=True),
        weight_panel,
        preferred_element_type=f32,
    )
    grad_parts = lax.dot_general(
        out_grad, weight_panel, (((1,), (1,)), ((), ())), preferred_element_type=f32
    )
    grad_norm = lax.psum_scatter(grad_parts, "col", scatter_dimension=1, tiled=True)
    scaled = grad_norm.reshape(tok_rows, groups_loc, HG * DH) * gain_groups
    grad_attend = inv_rms * (scaled - normed * jnp.mean(scaled * normed, axis=-1, keepdims=True))
    grad_heads = grad_attend.reshape(tok_rows, heads_loc, DH)
    own_qg = jnp.einsum("tha,thb->hab", query_float, grad_heads, precision=highest)
    suffix = carried_in(own_qg, ("seq", "row"), True)
    value_scores = jnp.einsum("thd,shd->hts", grad_heads, value_float, precision=highest) * causal
    query_part = jnp.einsum("hts,shd->thd", value_scores, key_float, precision=highest)
    query_part = query_part + jnp.einsum("the,hde->thd", grad_heads, prefix, precision=highest)
    key_part = jnp.einsum("hts,thd->shd", value_scores, query_float, precision=highest)
    key_part = key_part + jnp.einsum("shb,hab->sha", value_float, suffix, precision=highest)
    value_part = jnp.einsum("hts,the->she", key_scores, grad_heads, precision=highest)
    value_part = value_part + jnp.einsum("sha,hab->shb", key_float, suffix, precision=highest)
    query_grad = (query_part * score_scale).reshape(tok_rows, width_loc).astype(bf16)
    key_grad = (key_part * score_scale).reshape(tok_rows, width_loc).astype(bf16)
    value_grad = (value_part * score_scale).reshape(tok_rows, width_loc).astype(bf16)
    return (projected.astype(bf16), query_grad, key_grad, value_grad)


def row_swap(x):
    return lax.ppermute(x, "row", [(0, 1), (1, 0)])


def col_flip(x, bits):
    return lax.ppermute(x, "col", [(i, i ^ bits) for i in range(lax.axis_size("col"))])


def seq_shift(x, step):
    count = lax.axis_size("seq")
    return lax.ppermute(x, "seq", [(i, i + step) for i in range(count) if 0 <= i + step < count])


def seq_rotate(x):
    count = lax.axis_size("seq")
    return lax.ppermute(x, "seq", [(i, (i + 1) % count) for i in range(count)])


def shifts(state, sign):
    sent = state.astype(bf16)
    return [seq_shift(sent, sign * hop) for hop in range(1, lax.axis_size("seq"))]


def sum_of(parts):
    total = parts[0].astype(f32)
    for part in parts[1:]:
        total = total + part.astype(f32)
    return total


def dot(spec, a, b):
    return jnp.einsum(spec, a.astype(bf16), b.astype(bf16), preferred_element_type=f32)


class Fetch:
    def __init__(self, value):
        self.value = value


def block_of(shape):
    return pl.BlockSpec(tuple(shape), lambda: (0,) * len(shape))


def call(body, name, outs, place, ins, after=(), store=False):
    whole = pl.BlockSpec(memory_space=pltpu.VMEM)
    in_specs = [block_of(x.value.shape) if isinstance(x, Fetch) else whole for x in ins]
    ins = [x.value if isinstance(x, Fetch) else x for x in ins]
    anywhere = pl.BlockSpec(memory_space=pl.ANY)
    n_in, n_after = len(ins), len(after)

    def kernel(place_ref, *refs):
        body(place_ref, *refs[:n_in], *refs[n_in + n_after :])

    return pl.pallas_call(
        kernel,
        name=name,
        out_shape=[jax.ShapeDtypeStruct(shape, dtype) for shape, dtype in outs],
        in_specs=[pl.BlockSpec(memory_space=pltpu.SMEM)] + in_specs + [anywhere] * n_after,
        out_specs=[block_of(shape) if store else whole for shape, _ in outs],
        cost_estimate=pl.CostEstimate(flops=6 * 10**9 if name in ("local_grads", "back_state", "scale_grad") else 1, bytes_accessed=1, transcendentals=0),
        compiler_params=pltpu.CompilerParams(vmem_limit_bytes=40 * 2**20),
    )(place, *ins, *after)


def mm(a, b, ca, cb):
    return lax.dot_general(a, b, (((ca,), (cb,)), ((), ())), preferred_element_type=f32)


def half_of(ref, which, half):
    return ref[:, pl.ds(pl.multiple_of(which * half, DH), half)]


def head_of(ref, got, which, half, h):
    own = ref[:, pl.ds(pl.multiple_of(which * half + h * DH, DH), DH)]
    return jnp.concatenate([own, got[:, h * DH : (h + 1) * DH]], 0)


def swapped(x):
    tok = x.shape[0] // 2
    return jnp.concatenate([x[tok:], x[:tok]], 0)


def causal_mask(r, tok):
    def spot(axis):
        i = lax.broadcasted_iota(jnp.int32, (2 * tok, 2 * tok), axis)
        return jnp.where(i < tok, i + r * tok, i - r * tok)

    return spot(0) >= spot(1)


def total_of(parts, h):
    total = parts[0][h].astype(f32)
    for part in parts[1:]:
        total = total + part[h].astype(f32)
    return total.astype(bf16)


def head_split(query_input, key_input, value_input, norm_gain, out_weight, out_grad):
    score_scale = DH ** (-0.5)
    tok = query_input.shape[0]
    width = query_input.shape[1]
    half = width // 2
    heads = half // DH
    n_seq = lax.axis_size("seq")
    n_col = lax.axis_size("col")
    z = lax.axis_index("seq")
    r = lax.axis_index("row")
    c = lax.axis_index("col")

    held = []
    start = 0
    for count in CHUNK_HEADS:
        rows = count * DH
        blocks = [out_weight[start : start + rows]]
        for _ in range(n_seq - 1):
            blocks.append(seq_rotate(blocks[-1]))
        held.append(blocks)
        start += rows

    def halves_swapped(x):
        return jnp.concatenate([x[tok:], x[:tok]])

    def mine(x):
        return lax.dynamic_slice_in_dim(x, r * half, half, 1)

    def other(x):
        return lax.dynamic_slice_in_dim(x, (1 - r) * half, half, 1)

    qkv = (query_input, key_input, value_input)
    got = row_swap(jnp.stack([other(x) for x in qkv]))
    q, k, v = [
        jnp.concatenate([mine(x), got[i]], 0).reshape(2 * tok, heads, DH) for i, x in enumerate(qkv)
    ]
    grads = jnp.concatenate([out_grad, row_swap(out_grad)], 0)
    gain = lax.dynamic_slice_in_dim(norm_gain, r * half, half, 0)

    place = lax.broadcasted_iota(jnp.int32, (2 * tok, 1), 0)
    place = jnp.where(place < tok, place + r * tok, place - tok + (1 - r) * tok)
    causal = place >= place.reshape(1, 2 * tok)

    own_kv = dot("tha,thb->hab", k, v)
    prefix_parts = shifts(own_kv, 1)
    prefix = sum_of(prefix_parts)
    key_scores = jnp.where(causal, dot("thd,shd->hts", q, k), 0.0).astype(bf16)
    attend = dot("hts,shd->thd", key_scores, v) + dot("thd,hde->the", q, prefix)
    attend = attend.reshape(2 * tok, half) * score_scale
    squares = jnp.sum(attend * attend, axis=-1)
    squares = squares + halves_swapped(row_swap(squares))
    inv_rms = lax.rsqrt(squares * (1.0 / width) + norm_eps)[:, None]
    normed = attend * inv_rms
    normalized = (normed * gain).astype(bf16)

    pieces = []
    start = 0
    for count, blocks in zip(CHUNK_HEADS, held):
        parts = [
            lax.dot_general(grads, w, (((1,), (1,)), ((), ())), preferred_element_type=f32)
            for w in blocks
        ]

        def group(g):
            out = parts[0]
            for s in range(1, n_seq):
                out = jnp.where((z - g) % n_seq == s, parts[s], out)
            return out

        piece = group(c)
        for bits in range(1, n_col):
            piece = piece + col_flip(group(c ^ bits).astype(bf16), bits).astype(f32)
        pieces.append(piece)
        start += count

    feats = [normalized] + [col_flip(normalized, bits) for bits in range(1, n_col)]

    def features(g):
        out = feats[0]
        for bits in range(1, n_col):
            out = jnp.where(c ^ g == bits, feats[bits], out)
        return out

    partial = 0.0
    for s in range(n_seq):
        weight = jnp.concatenate([blocks[s] for blocks in held], 0)
        partial = partial + jnp.dot(
            features((z - s) % n_seq), weight, preferred_element_type=f32
        )
    scale = score_scale
    both = 2 * tok
    outs_loc = out_weight.shape[1]
    place = jnp.stack([z, r, c]).astype(jnp.int32)

    def scale_grad(s, *refs):
        grads, (gain, attend, inv_rms, scaled, inner) = refs[:heads], refs[heads:]
        total = 0.0
        for h in range(heads):
            cols = slice(h * DH, (h + 1) * DH)
            grad = grads[h][...] * gain[:, cols]
            scaled[:, cols] = grad
            normed = attend[:, cols] * inv_rms[...]
            total = total + jnp.sum(grad * normed, axis=1, keepdims=True)
        inner[...] = total

    scaled, inner = call(
        scale_grad,
        "scale_grad",
        [((both, half), f32), ((both, 1), f32)],
        place,
        [*pieces, gain.reshape(1, half), attend, inv_rms],
    )

    def back_state(s, scaled, inner, inner_got, attend, inv_rms, q, got, grad, state):
        mean = (inner[...] + swapped(inner_got[...])) * (1.0 / width)
        inv = inv_rms[...]
        value = (inv * (scaled[...] - attend[...] * inv * mean)).astype(bf16)
        grad[...] = value
        for h in range(heads):
            queries = head_of(q, got.at[0], s[1], half, h)
            state[h] = mm(queries, value[:, h * DH : (h + 1) * DH], 0, 0).astype(bf16)

    grad, state = call(
        back_state,
        "back_state",
        [((both, half), bf16), ((heads, DH, DH), bf16)],
        place,
        [scaled, inner, row_swap(inner), attend, inv_rms, query_input, got],
    )
    suffix = shifts(state, -1)

    def local_grads(s, q, k, v, got, grad, *refs):
        *prefix, dq_own, dq_other, own, other = refs
        mask = causal_mask(s[1], tok)
        for h in range(heads):
            cols = slice(h * DH, (h + 1) * DH)
            queries = head_of(q, got.at[0], s[1], half, h)
            keys = head_of(k, got.at[1], s[1], half, h)
            vals = head_of(v, got.at[2], s[1], half, h)
            grads = grad[:, cols]
            key_scores = jnp.where(mask, mm(queries, keys, 1, 1), 0.0).astype(bf16)
            value_scores = jnp.where(mask, mm(grads, vals, 1, 1), 0.0).astype(bf16)
            dq = mm(value_scores, keys, 1, 0) + mm(grads, total_of(prefix, h), 1, 1)
            dq = (dq * scale).astype(bf16)
            dq_own[:, cols] = dq[:tok]
            dq_other[:, cols] = dq[tok:]
            dk = mm(value_scores, queries, 0, 0)
            dv = mm(key_scores, grads, 0, 0)
            for i, x in enumerate((dk, dv)):
                own[i, :, cols] = x[:tok]
                other[i, :, cols] = x[tok:]

    dq_own, dq_other, kv_own, kv_other = call(
        local_grads,
        "local_grads",
        [((tok, half), bf16)] * 2 + [((2, tok, half), f32)] * 2,
        place,
        [query_input, key_input, value_input, got, grad, *prefix_parts],
    )
    kv_got = row_swap(kv_other)

    def finish_early(s, own, other, dq_own, dq_other, out, dq, token):
        token[...] = jnp.zeros_like(token)
        out[...] = (own[:tok] + other[...]).astype(bf16)
        dq[:, pl.ds(pl.multiple_of(s[1] * half, DH), half)] = dq_own[...]
        dq[:, pl.ds(pl.multiple_of((1 - s[1]) * half, DH), half)] = dq_other[...]

    projected, query_grad, token = call(
        finish_early,
        "finish_early",
        [((tok, outs_loc), bf16), ((tok, width), bf16), ((8, DH), f32)],
        place,
        [partial, row_swap(partial[tok:]), dq_own, row_swap(dq_other)],
        store=True,
    )

    def sum_later(s, *refs):
        *parts, total = refs
        for h in range(heads):
            total[h] = total_of(parts, h)

    (later,) = call(
        sum_later,
        "sum_later",
        [((heads, DH, DH), bf16)],
        place,
        suffix,
    )

    def far_grads(s, k, v, kv_own, kv_got, later, later_got, token, key_grad, value_grad):
        for local, state, which in ((kv_own, later, s[1]), (kv_got, later_got, 1 - s[1])):
            for h in range(heads):
                cols = slice(h * DH, (h + 1) * DH)
                place_cols = pl.ds(pl.multiple_of(which * half + h * DH, DH), DH)
                dk = local[0, :, cols] + mm(v[:, place_cols], state[h], 1, 1)
                dv = local[1, :, cols] + mm(k[:, place_cols], state[h], 1, 0)
                key_grad[:, place_cols] = (dk * scale).astype(bf16)
                value_grad[:, place_cols] = (dv * scale).astype(bf16)

    key_grad, value_grad = call(
        far_grads,
        "far_grads",
        [((tok, width), bf16)] * 2,
        place,
        [key_input, value_input, kv_own, kv_got, later, row_swap(later), token],
        store=True,
    )
    return (projected, query_grad, key_grad, value_grad)


def solution(mesh):
    sizes = dict(mesh.shape)

    def per_device(query_input, key_input, value_input, norm_gain, out_weight, out_grad):
        width = query_input.shape[1]
        fits = (
            sizes["row"] == 2
            and sizes["seq"] == sizes["col"] == 4
            and width == HG * DH
            and 2 * out_weight.shape[0] == width
        )
        plan = head_split if fits else general
        return plan(query_input, key_input, value_input, norm_gain, out_weight, out_grad)

    in_specs = (
        P(("seq", "row"), "col"),
        P(("seq", "row"), "col"),
        P(("seq", "row"), "col"),
        P("col"),
        P(("seq", "row"), "col"),
        P(("seq", "row"), "col"),
    )
    out_specs = (
        P(("seq", "row"), "col"),
        P(("seq", "row"), "col"),
        P(("seq", "row"), "col"),
        P(("seq", "row"), "col"),
    )
    return jax.shard_map(
        per_device, mesh=mesh, in_specs=in_specs, out_specs=out_specs, check_vma=False
    )
```
